32 devices in a mesh: groups: 2 (over x), seq: 16 (over z, y, core).
Axes of the slice: x: 2, y: 2, z: 4, core: 2. Of those that a mesh axis runs over, the one named last changes fastest.
Arguments:
- x_in: bfloat16 [4096, 4096], P(('groups', 'seq')), parts along dimension 0, may hold values from -6 to 6
- bc_in: bfloat16 [4096, 1024], P(('groups', 'seq')), parts along dimension 0, may hold values from -6 to 6
- z_in: bfloat16 [4096, 4096], P(('groups', 'seq')), parts along dimension 0, may hold values from -6 to 6
- dt_in: bfloat16 [4096, 128], P(('groups', 'seq')), parts along dimension 0, may hold values from -4 to 4
- conv_weight: float32 [4, 5120], replicated, may hold values from -3 to 3
- conv_bias: float32 [5120], replicated, may hold values from -3 to 3
- dt_bias: float32 [128], replicated, may hold values from -4 to -2
- a_log: float32 [128], replicated, may hold values from -11.5 to 0
- d_skip: float32 [128], replicated, may hold values from 0.5 to 1.5
- norm_gain: float32 [4096], replicated, may hold values from 0.5 to 1.5
- conv_cache: bfloat16 [6, 5120], P('groups'), parts along dimension 0, may hold values from -6 to 6
- cache_state: float32 [256, 32, 64], P('groups'), parts along dimension 0, may hold values from -6 to 6
- lengths: int32 [2], P('groups'), parts along dimension 0, may hold values from 1924 to 2048
Outputs:
- mixed: bfloat16 [4096, 4096], P(('groups', 'seq')), parts along dimension 0
- final_state: float32 [256, 32, 64], P(('groups', 'seq')), parts along dimension 0
The draws below stay inside these ranges and needn't reach their ends.
There are 2 independent parts, one for each index of `groups`. The reference program is written for one: setup_inputs(seed, part) draws one part's arguments, and reference() takes and returns one part's arrays. A program takes and returns all parts, laid end to end along the dimension named above; an argument that names none is the same for every part. Nothing has to cross between parts.
All inputs are finite; a program needn't handle non-finite values.
Results may differ from the reference program's by a relative error of at most 0.0085.
Values may be sent and summed in bfloat16 or wider, within the bound.
A program may use at most 64 MiB of HBM per device.

```python
import jax
import jax.numpy as jnp
from jax import lax

HEADS = 128
HEAD_DIM = 32
STATE = 64
GROUPS = 8
CONV_W = 4
TOK_DEV = 128
TOKENS = 2048
INNER = 4096
CONV_CH = 5120


def level_of(key, extent, split, smallest, top_value):
    level = 1.0
    for dim, shards_of in split:
        draws = jax.random.uniform(jax.random.fold_in(jax.random.fold_in(key, 6), dim), (shards_of,), jnp.float32, smallest / len(split), top_value / len(split))
        level = level * jnp.repeat(jnp.exp(draws), extent[dim] // shards_of).reshape((-1,) + (1,) * (len(extent) - 1 - dim))
    return level


def gaussian(key, dims, deviation, reach, shards=(), held_as=jnp.bfloat16):
    factor_of = level_of(key, dims, shards, -0.22, 0.18) if shards else 1.0
    array = jax.random.normal(key, dims, jnp.float32) * deviation * factor_of
    return jnp.minimum(jnp.maximum(array, -reach), reach).astype(held_as)


def setup_inputs(seed: int = 0, part: int = 0) -> dict:
    key_of = jax.random.split(jax.random.key(seed), 14)
    own_keys = jax.random.split(jax.random.fold_in(key_of[13], part), 14)
    return {
        "x_in": gaussian(own_keys[0], (TOKENS, INNER), 1.0, 6.0, ((0, 16),)),
        "bc_in": gaussian(own_keys[1], (TOKENS, 2 * GROUPS * STATE), 1.0, 6.0, ((0, 16),)),
        "z_in": gaussian(own_keys[2], (TOKENS, INNER), 1.0, 6.0, ((0, 16),)),
        "dt_in": gaussian(own_keys[3], (TOKENS, HEADS), 1.0, 4.0, ((0, 16),)),
        "conv_weight": gaussian(key_of[4], (CONV_W, CONV_CH), CONV_W ** -0.5, 3.0, (), jnp.float32),
        "conv_bias": gaussian(key_of[5], (CONV_CH,), 0.5, 3.0, (), jnp.float32),
        "dt_bias": jnp.clip(jax.random.uniform(key_of[6], (HEADS,), jnp.float32, -4.0, -2.0), -4.0, -2.0),
        "a_log": jnp.clip(jax.random.uniform(key_of[7], (HEADS,), jnp.float32, -11.5, 0.0), -11.5, 0.0),
        "d_skip": jnp.clip(jax.random.uniform(key_of[8], (HEADS,), jnp.float32, 0.5, 1.5), 0.5, 1.5),
        "norm_gain": jnp.clip(1.0 + 0.1 * jax.random.normal(key_of[9], (INNER,), jnp.float32), 0.5, 1.5),
        "conv_cache": gaussian(own_keys[10], (CONV_W - 1, CONV_CH), 1.0, 6.0),
        "cache_state": gaussian(own_keys[11], (HEADS, HEAD_DIM, STATE), 1.0, 6.0, (), jnp.float32),
        "lengths": jax.random.randint(own_keys[12], (1,), TOKENS - TOK_DEV + CONV_W, TOKENS + 1).astype(jnp.int32),
    }


def conv_silu(extended, conv_weight, conv_bias, count):
    total = jnp.zeros((count, extended.shape[1]), jnp.float32) + conv_bias[None, :]
    for offset in range(CONV_W):
        total = total + extended[offset:offset + count].astype(jnp.float32) * conv_weight[offset][None, :]
    return jax.nn.silu(total).astype(jnp.bfloat16)

def block_step(state, pieces, decay_rate, d_skip):
    x_block, b_block, c_block, dt_block = pieces
    per_group = HEADS // GROUPS
    block_len = x_block.shape[0]
    hi_prec = lax.Precision.HIGHEST
    cum_rate = jnp.cumsum(dt_block * decay_rate[None, :], axis=0)
    lower_mask = jnp.arange(block_len)[:, None] >= jnp.arange(block_len)[None, :]
    gap_rate = cum_rate.T[:, :, None] - cum_rate.T[:, None, :]
    decay = jnp.exp(jnp.where(lower_mask[None], gap_rate, -1e+30))
    c_dot_b = jnp.einsum('tgn,sgn->gts', c_block.astype(jnp.float32), b_block.astype(jnp.float32), precision=hi_prec)
    c_dot_b = jnp.repeat(c_dot_b, per_group, axis=0)
    weight = lax.optimization_barrier((c_dot_b * decay * dt_block.T[:, None, :]).astype(jnp.bfloat16))
    x_float = x_block.astype(jnp.float32)
    y_diag = jnp.einsum('hts,shp->thp', weight.astype(jnp.float32), x_float, precision=hi_prec)
    c_heads = jnp.repeat(c_block.astype(jnp.float32), per_group, axis=1)
    y_enter = jnp.exp(cum_rate)[:, :, None] * jnp.einsum('thn,hpn->thp', c_heads, state, precision=hi_prec)
    y_block = y_diag + y_enter + d_skip[None, :, None] * x_float
    tail = jnp.exp(cum_rate[-1][None, :] - cum_rate) * dt_block
    b_heads = jnp.repeat(b_block.astype(jnp.float32), per_group, axis=1)
    b_weighted = lax.optimization_barrier((b_heads * tail[:, :, None]).astype(jnp.bfloat16))
    local = jnp.einsum('shp,shn->hpn', x_float, b_weighted.astype(jnp.float32), precision=hi_prec)
    new_state = jnp.exp(cum_rate[-1])[:, None, None] * state + local
    return (new_state, y_block)

def reference(x_in, bc_in, z_in, dt_in, conv_weight, conv_bias, dt_bias, a_log, d_skip, norm_gain, conv_cache, cache_state, lengths):
    inputs = jnp.concatenate([x_in, bc_in], axis=1)
    extended = jnp.concatenate([conv_cache, inputs], axis=0)
    convolved = conv_silu(extended, conv_weight, conv_bias, TOKENS)
    x_conv = convolved[:, :INNER].reshape(TOKENS, HEADS, HEAD_DIM)
    b_conv = convolved[:, INNER:INNER + GROUPS * STATE].reshape(TOKENS, GROUPS, STATE)
    c_conv = convolved[:, INNER + GROUPS * STATE:].reshape(TOKENS, GROUPS, STATE)
    live = (jnp.arange(TOKENS) < lengths[0]).astype(jnp.float32)
    step_size = jax.nn.softplus(dt_in.astype(jnp.float32) + dt_bias[None, :]) * live[:, None]
    decay_rate = -jnp.exp(a_log)
    blocks = TOKENS // TOK_DEV
    pieces = (x_conv.reshape(blocks, TOK_DEV, HEADS, HEAD_DIM), b_conv.reshape(blocks, TOK_DEV, GROUPS, STATE), c_conv.reshape(blocks, TOK_DEV, GROUPS, STATE), step_size.reshape(blocks, TOK_DEV, HEADS))

    def scan_step(state, piece):
        return block_step(state, piece, decay_rate, d_skip)
    final_state, y_blocks = lax.scan(scan_step, cache_state, pieces)
    y_out = lax.optimization_barrier((y_blocks.reshape(TOKENS, INNER) * live[:, None]).astype(jnp.bfloat16))
    gated = y_out.astype(jnp.float32) * jax.nn.silu(z_in.astype(jnp.float32))
    grouped = gated.reshape(TOKENS, GROUPS, INNER // GROUPS)
    scale = lax.rsqrt(lax.optimization_barrier(jnp.mean(grouped * grouped, axis=-1, keepdims=True)) + 1e-05)
    mixed = (grouped * scale).reshape(TOKENS, INNER) * norm_gain[None, :]
    return (mixed.astype(jnp.bfloat16), final_state)
```

```python
import functools

import jax
import jax.numpy as jnp
from jax import lax
from jax.experimental import pallas as pl
from jax.experimental.pallas import tpu as pltpu
from jax.sharding import PartitionSpec as P

GROUPS = 8
MESH = pl.DeviceIdType.MESH
F32 = jnp.float32
BF16 = jnp.bfloat16
HIGHEST = lax.Precision.HIGHEST


def iota(shape, dim):
    return lax.broadcasted_iota(jnp.int32, shape, dim)


def split_bf16(value):
    high = value.astype(BF16)
    return high, (value - high.astype(F32)).astype(BF16)


def kernel(
    devices,
    len_ref,
    x_ref,
    bc_ref,
    z_ref,
    dt_ref,
    cw_ref,
    cb_ref,
    head_ref,
    skip_ref,
    gain_ref,
    ccache_ref,
    cstate_ref,
    out_ref,
    final_ref,
    ext,
    xc,
    bt,
    cs,
    ypart,
    factors,
    rim_send,
    rim_recv,
    cache_buf,
    ends,
    dsend,
    drecv,
    dec,
    dmine,
    local,
    pbuf,
    asend,
    abuf,
    esend,
    ebuf,
    psend,
    enter,
    rim_sem,
    cache_sem,
    end_sem,
    d_sems,
    p_sem,
    a_sems,
    e_sems,
    n_sems,
):
    tok, inner = x_ref.shape
    heads = dt_ref.shape[1]
    head_dim = inner // heads
    state = bt.shape[1]
    width = inner // GROUPS
    per_group = heads // GROUPS
    chips = devices // 2
    share = heads // devices
    own = share * head_dim
    half = tok // 2
    owners = per_group // share
    rim_rows = ccache_ref.shape[0]
    pad = ext.shape[0] - tok

    me = lax.axis_index("seq")
    core = lax.rem(me, 2)
    chip = me // 2
    partner = chip * 2 + 1 - core
    after = lax.rem(me + 1, devices)
    before = lax.rem(me + devices - 1, devices)
    far = lax.rem(me + devices + 2 * core - 1, devices)
    even = core == 0

    def remote(src, dst, send, recv, where):
        return pltpu.make_async_remote_copy(
            src_ref=src,
            dst_ref=dst,
            send_sem=send,
            recv_sem=recv,
            device_id={"seq": where},
            device_id_type=MESH,
        )

    def peer_of(d):
        other = lax.rem(chip + d, chips)
        return other, other * 2 + core

    cache_copy = pltpu.make_async_copy(
        cstate_ref.at[pl.ds(pl.multiple_of(me * own, own), own)], cache_buf, cache_sem
    )
    cache_copy.start()

    barrier = pltpu.get_barrier_semaphore()
    for other in (partner, far):
        pl.semaphore_signal(barrier, inc=1, device_id={"seq": other}, device_id_type=MESH)

    def greet(d, carry):
        pl.semaphore_signal(
            barrier, inc=1, device_id={"seq": peer_of(d)[1]}, device_id_type=MESH
        )
        return carry

    lax.fori_loop(1, chips, greet, 0)
    rim_send[:, :inner] = x_ref[tok - rim_rows :, :]
    rim_send[:, inner:] = bc_ref[tok - rim_rows :, :]
    pl.semaphore_wait(barrier, chips + 1)

    rim_copy = remote(rim_send, rim_recv, rim_sem.at[0], rim_sem.at[1], after)
    rim_copy.start()

    live = (iota((tok, 1), 0) + me * tok < len_ref[0]).astype(F32)
    raw = dt_ref[...].astype(F32) + head_ref[0:1, :]
    step = (jnp.maximum(raw, 0.0) + jnp.log1p(jnp.exp(-jnp.abs(raw)))) * live
    rate = -jnp.exp(head_ref[1:2, :]) * step
    lower = (iota((tok, tok), 0) >= iota((tok, tok), 1)).astype(F32)
    cum = jnp.dot(lower, rate, precision=HIGHEST, preferred_element_type=F32)
    end = cum[tok - 1 : tok, :]
    ends[0] = jnp.broadcast_to(end, ends.shape[1:])
    end_copy = remote(ends.at[0], ends.at[1], end_sem.at[0], end_sem.at[1], partner)
    end_copy.start()
    first_mid = cum[half // 2 - 1 : half // 2, :]
    second_mid = cum[half + half // 2 - 1 : half + half // 2, :]
    middle = jnp.where(iota((tok, 1), 0) < half, first_mid, second_mid)
    pieces = (
        jnp.exp(end - cum) * step,
        jnp.exp(cum - middle),
        jnp.exp(middle - cum) * step,
        jnp.exp(cum),
        jnp.exp(second_mid - cum[:half]) * step[:half],
    )
    row = 0
    for piece in pieces:
        high, low = split_bf16(piece)
        factors[row : row + piece.shape[0], :heads] = high
        factors[row : row + piece.shape[0], heads:] = low
        row += piece.shape[0]

    def expand(rows, group):
        hit = lax.rem(iota((2 * heads, width), 0), heads) == (
            group * per_group + iota((2 * heads, width), 1) // head_dim
        )
        return jnp.dot(rows, hit.astype(F32).astype(BF16), preferred_element_type=F32)

    ext[pad:, :inner] = x_ref[...].astype(F32)
    ext[pad:, inner:] = bc_ref[...].astype(F32)

    end_copy.wait()
    pair = ends[0] + ends[1]
    dsend[...] = pair
    drecv[chip] = pair

    def send_decay(d, carry):
        other, where = peer_of(d)
        remote(dsend, drecv.at[chip], d_sems.at[0, other], d_sems.at[1, chip], where).start()
        return carry

    lax.fori_loop(1, chips, send_decay, 0)

    rim_copy.wait()
    first = me == 0
    rim = jnp.where(first, ccache_ref[...].astype(F32), rim_recv[...].astype(F32))
    ext[pad - rim_rows : pad, :] = rim

    def conv(columns):
        total = jnp.broadcast_to(cb_ref[0:1, columns], (tok, columns.size))
        for k in range(rim_rows + 1):
            total = total + ext[pl.ds(pad - rim_rows + k, tok), columns] * cw_ref[k : k + 1, columns]
        return total * jax.nn.sigmoid(total)

    span = GROUPS * state
    b_all = conv(pl.ds(inner, span)).T
    for g in range(GROUPS):
        bt[g] = b_all[g * state : (g + 1) * state].astype(BF16)
    c_all = conv(pl.ds(inner + span, span)).astype(BF16)
    for g in range(GROUPS):
        cs[g] = c_all[:, g * state : (g + 1) * state]

    def columns_of(group):
        return pl.ds(pl.multiple_of(group * width, width), width)

    def local_step(group, carry):
        columns = columns_of(group)
        x = conv(columns).astype(BF16)
        xc[:, columns] = x
        tail = expand(factors[:tok, :], group)
        scaled = (x.astype(F32) * tail).astype(BF16)
        sums = jnp.dot(bt[group], scaled, preferred_element_type=F32).astype(BF16)
        for k in range(owners):
            local[k % 2, group * (owners // 2) + k // 2] = sums[:, k * own : (k + 1) * own]
        return carry

    lax.fori_loop(0, GROUPS, local_step, 0)
    p_copy = remote(local.at[1 - core], pbuf, p_sem.at[0], p_sem.at[1], partner)
    p_copy.start()

    def diag_step(group, carry):
        columns = columns_of(group)
        grown = expand(factors[tok : 3 * tok, :], group)
        grown_off = expand(factors[4 * tok : 4 * tok + half, :], group)
        x = xc[:, columns].astype(F32)
        scaled = (x * grown[tok:]).astype(BF16)
        scaled_off = (x[:half] * grown_off).astype(BF16)
        inner_cb = jnp.dot(cs[group], bt[group], preferred_element_type=F32)
        inner_cb = jnp.where(iota((tok, tok), 0) >= iota((tok, tok), 1), inner_cb, 0.0)
        inner_cb = inner_cb.astype(BF16)
        top = jnp.dot(inner_cb[:half, :half], scaled[:half], preferred_element_type=F32)
        bottom = jnp.dot(
            inner_cb[half:],
            jnp.concatenate([scaled_off, scaled[half:]], axis=0),
            preferred_element_type=F32,
        )
        skip = skip_ref[0:1, columns]
        ypart[:half, columns] = top * grown[:half] + skip * x[:half]
        ypart[half:, columns] = bottom * grown[half:tok] + skip * x[half:]
        return carry

    lax.fori_loop(0, 2, diag_step, 0)

    both = jnp.concatenate([ends[0], ends[1]], axis=0)
    both = jnp.exp(both)

    def widen(o, carry):
        hit = iota((heads, own), 0) == (
            (o * 2 + core) * share + iota((heads, own), 1) // head_dim
        )
        dec[o] = jnp.dot(both, hit.astype(F32), precision=HIGHEST, preferred_element_type=F32)
        return carry

    lax.fori_loop(0, chips, widen, 0)

    def block_decay(o, of_even):
        mine = dec[o, 0:1, :]
        theirs = dec[o, ends.shape[1] : ends.shape[1] + 1, :]
        return jnp.where(even == of_even, mine, theirs)

    def block_local(o, of_even):
        return jnp.where(even == of_even, local[core, o].astype(F32), pbuf[o].astype(F32))

    p_copy.wait()

    def a_copy(other, where):
        return remote(
            asend.at[other], abuf.at[chip], a_sems.at[0, other], a_sems.at[1, chip], where
        )

    def send_pair(d, carry):
        other, where = peer_of(d)
        joined = block_decay(other, False) * block_local(other, True) + block_local(other, False)
        asend[other] = joined.astype(BF16)
        a_copy(other, where).start()
        return carry

    lax.fori_loop(1, chips, send_pair, 0)
    joined = block_decay(chip, False) * block_local(chip, True) + block_local(chip, False)
    abuf[chip] = joined.astype(BF16)

    lax.fori_loop(2, 6, diag_step, 0)

    def wait_decay(d, carry):
        other, where = peer_of(d)
        copy = remote(dsend, drecv.at[other], d_sems.at[0, other], d_sems.at[1, other], where)
        copy.wait()
        return carry

    lax.fori_loop(1, chips, wait_decay, 0)
    hit = iota((heads, own), 0) == (me * share + iota((heads, own), 1) // head_dim)
    dmine[...] = jnp.dot(
        jnp.exp(drecv[:, 0, :]), hit.astype(F32), precision=HIGHEST, preferred_element_type=F32
    )
    cache_copy.wait()

    def wait_pair(d, carry):
        other, where = peer_of(d)
        copy = remote(
            asend.at[other], abuf.at[other], a_sems.at[0, other], a_sems.at[1, other], where
        )
        copy.wait()
        return carry

    lax.fori_loop(1, chips, wait_pair, 0)

    def scan_step(s, carried):
        esend[s] = carried.astype(BF16)
        return dmine[pl.ds(s, 1), :] * carried + abuf[s].astype(F32)

    final = lax.fori_loop(0, chips, scan_step, cache_buf[...].T)

    def send_enter(d, carry):
        other, where = peer_of(d)
        remote(
            esend.at[other], ebuf.at[chip], e_sems.at[0, other], e_sems.at[1, chip], where
        ).start()
        return carry

    lax.fori_loop(1, chips, send_enter, 0)
    final_ref[...] = final.T
    ebuf[chip] = esend[chip]

    lax.fori_loop(6, GROUPS, diag_step, 0)

    def pass_on(o):
        at_even = ebuf[o]
        at_odd = block_decay(o, True) * at_even.astype(F32) + block_local(o, True)
        at_odd = at_odd.astype(BF16)
        enter[core, o] = jnp.where(even, at_even, at_odd)
        psend[o] = jnp.where(even, at_odd, at_even)
        remote(
            psend.at[o], enter.at[core, o], n_sems.at[0, o], n_sems.at[1, o], partner
        ).start()

    pass_on(chip)

    def wait_enter(d, carry):
        other, where = peer_of(d)
        copy = remote(
            esend.at[other], ebuf.at[other], e_sems.at[0, other], e_sems.at[1, other], where
        )
        copy.wait()
        pass_on(other)
        return carry

    lax.fori_loop(1, chips, wait_enter, 0)

    def wait_partner(o, carry):
        remote(
            psend.at[o], enter.at[1 - core, o], n_sems.at[0, o], n_sems.at[1, o], partner
        ).wait()
        return carry

    lax.fori_loop(0, chips, wait_partner, 0)

    def gate_step(group, carry):
        columns = columns_of(group)
        entering = jnp.concatenate(
            [enter[k % 2, group * (owners // 2) + k // 2] for k in range(owners)], axis=1
        )
        carried = expand(factors[3 * tok : 4 * tok, :], group)
        y = ypart[:, columns] + carried * jnp.dot(
            cs[group], entering, preferred_element_type=F32
        )
        y = (y * live).astype(BF16).astype(F32)
        z = z_ref[:, columns].astype(F32)
        gated = y * (z * jax.nn.sigmoid(z))
        scale = lax.rsqrt(jnp.mean(gated * gated, axis=-1, keepdims=True) + 1e-05)
        out_ref[:, columns] = (gated * scale * gain_ref[0:1, columns]).astype(BF16)
        return carry

    lax.fori_loop(0, GROUPS, gate_step, 0)


def body(
    devices,
    x_in,
    bc_in,
    z_in,
    dt_in,
    conv_weight,
    conv_bias,
    dt_bias,
    a_log,
    d_skip,
    norm_gain,
    conv_cache,
    cache_state,
    lengths,
):
    tok, inner = x_in.shape
    wide = inner + bc_in.shape[1]
    heads, head_dim, state = cache_state.shape
    chips = devices // 2
    share = heads // devices
    own = share * head_dim
    rim_rows = conv_cache.shape[0]
    vmem = pl.BlockSpec(memory_space=pltpu.VMEM)
    dma = pltpu.SemaphoreType.DMA
    mixed, final = pl.pallas_call(
        functools.partial(kernel, devices),
        out_shape=(
            jax.ShapeDtypeStruct((tok, inner), BF16),
            jax.ShapeDtypeStruct((own, state), F32),
        ),
        in_specs=[pl.BlockSpec(memory_space=pltpu.SMEM)]
        + [vmem] * 10
        + [pl.BlockSpec(memory_space=pl.ANY)],
        out_specs=(vmem, vmem),
        scratch_shapes=[
            pltpu.VMEM((tok + 8, wide), F32),
            pltpu.VMEM((tok, inner), BF16),
            pltpu.VMEM((GROUPS, state, tok), BF16),
            pltpu.VMEM((GROUPS, tok, state), BF16),
            pltpu.VMEM((tok, inner), F32),
            pltpu.VMEM((4 * tok + tok // 2, 2 * heads), BF16),
            pltpu.VMEM((rim_rows, wide), BF16),
            pltpu.VMEM((rim_rows, wide), BF16),
            pltpu.VMEM((own, state), F32),
            pltpu.VMEM((2, 8, heads), F32),
            pltpu.VMEM((8, heads), F32),
            pltpu.VMEM((chips, 8, heads), F32),
            pltpu.VMEM((chips, 16, own), F32),
            pltpu.VMEM((chips, own), F32),
            pltpu.VMEM((2, chips, state, own), BF16),
            pltpu.VMEM((chips, state, own), BF16),
            pltpu.VMEM((chips, state, own), BF16),
            pltpu.VMEM((chips, state, own), BF16),
            pltpu.VMEM((chips, state, own), BF16),
            pltpu.VMEM((chips, state, own), BF16),
            pltpu.VMEM((chips, state, own), BF16),
            pltpu.VMEM((2, chips, state, own), BF16),
            dma((2,)),
            dma(()),
            dma((2,)),
            dma((2, chips)),
            dma((2,)),
            dma((2, chips)),
            dma((2, chips)),
            dma((2, chips)),
        ],
        compiler_params=pltpu.CompilerParams(
            collective_id=0, has_side_effects=True, vmem_limit_bytes=60 * 1024 * 1024
        ),
    )(
        lengths,
        x_in,
        bc_in,
        z_in,
        dt_in,
        conv_weight,
        conv_bias[None, :],
        jnp.stack([dt_bias, a_log]),
        jnp.repeat(d_skip, head_dim)[None, :],
        norm_gain[None, :],
        conv_cache,
        cache_state.reshape(heads * head_dim, state),
    )
    return mixed, final.reshape(share, head_dim, state)


def solution(mesh):
    tokens = P(("groups", "seq"), None)
    in_specs = (
        tokens,
        tokens,
        tokens,
        tokens,
        P(),
        P(),
        P(),
        P(),
        P(),
        P(),
        P("groups", None),
        P("groups", None, None),
        P("groups"),
    )
    out_specs = (tokens, P(("groups", "seq"), None, None))
    return jax.shard_map(
        functools.partial(body, mesh.shape["seq"]),
        mesh=mesh,
        in_specs=in_specs,
        out_specs=out_specs,
        check_vma=False,
    )
```

```python
import functools

import jax
import jax.numpy as jnp
from jax import lax
from jax.experimental import pallas as pl
from jax.experimental.pallas import tpu as pltpu
from jax.sharding import PartitionSpec as P

GROUPS = 8
MESH = pl.DeviceIdType.MESH
F32 = jnp.float32
BF16 = jnp.bfloat16
HIGHEST = lax.Precision.HIGHEST


def iota(shape, dim):
    return lax.broadcasted_iota(jnp.int32, shape, dim)


def split_bf16(value):
    high = value.astype(BF16)
    return high, (value - high.astype(F32)).astype(BF16)


def sigmoid(value):
    return 0.5 * jnp.tanh(0.5 * value) + 0.5


def kernel(
    devices,
    len_ref,
    x_ref,
    bc_ref,
    z_ref,
    dt_ref,
    cw_ref,
    cb_ref,
    bias_ref,
    log_ref,
    skip_ref,
    gain_ref,
    ccache_ref,
    cstate_ref,
    out_ref,
    final_ref,
    ext,
    xc,
    bt,
    cs,
    ypart,
    zgate,
    carried,
    hits,
    tails,
    factors,
    rim_send,
    rim_recv,
    cache_all,
    cache_buf,
    ends,
    dsend,
    drecv,
    dec,
    dmine,
    local,
    pbuf,
    asend,
    abuf,
    esend,
    ebuf,
    psend,
    enter,
    rim_sem,
    cache_sem,
    end_sem,
    d_sems,
    p_sems,
    a_sems,
    e_sems,
    n_sems,
):
    tok, inner = x_ref.shape
    heads = dt_ref.shape[1]
    head_dim = inner // heads
    state = bt.shape[1]
    width = inner // GROUPS
    per_group = heads // GROUPS
    chips = devices // 2
    share = heads // devices
    own = share * head_dim
    half = tok // 2
    owners = per_group // share
    per_chip = chips // GROUPS
    rim_rows = ccache_ref.shape[0]
    pad = ext.shape[0] - tok

    me = lax.axis_index("seq")
    core = lax.rem(me, 2)
    chip = me // 2
    partner = chip * 2 + 1 - core
    after = lax.rem(me + 1, devices)
    far = lax.rem(me + devices + 2 * core - 1, devices)
    even = core == 0
    home = chip // per_chip

    def remote(src, dst, sems, mine, theirs, where):
        return pltpu.make_async_remote_copy(
            src_ref=src,
            dst_ref=dst,
            send_sem=sems.at[0, mine],
            recv_sem=sems.at[1, theirs],
            device_id={"seq": where},
            device_id_type=MESH,
        )

    def peer_of(d):
        other = lax.rem(chip + d, chips)
        return other, other * 2 + core

    cache_copy = pltpu.make_async_copy(cstate_ref, cache_all, cache_sem)
    cache_copy.start()

    barrier = pltpu.get_barrier_semaphore()
    for other in (partner, far):
        pl.semaphore_signal(barrier, inc=1, device_id={"seq": other}, device_id_type=MESH)

    def greet(d, carry):
        pl.semaphore_signal(
            barrier, inc=1, device_id={"seq": peer_of(d)[1]}, device_id_type=MESH
        )
        return carry

    lax.fori_loop(1, chips, greet, 0)
    rim_send[:, :inner] = x_ref[tok - rim_rows :, :]
    rim_send[:, inner:] = bc_ref[tok - rim_rows :, :]

    live = (iota((tok, 1), 0) + me * tok < len_ref[0]).astype(F32)
    raw = dt_ref[...].astype(F32) + bias_ref[...]
    step = (jnp.maximum(raw, 0.0) + jnp.log1p(jnp.exp(-jnp.abs(raw)))) * live
    rate = -jnp.exp(log_ref[...]) * step
    lower = (iota((tok, tok), 0) >= iota((tok, tok), 1)).astype(F32)
    cum = jnp.dot(lower, rate, precision=HIGHEST, preferred_element_type=F32)
    end = cum[tok - 1 : tok, :]
    ends[0] = jnp.broadcast_to(end, ends.shape[1:])

    pl.semaphore_wait(barrier, chips + 1)
    rim_copy = remote(rim_send, rim_recv, rim_sem, 0, 0, after)
    rim_copy.start()
    end_copy = remote(ends.at[0], ends.at[1], end_sem, 0, 0, partner)
    end_copy.start()

    def keep(ref, row, piece):
        high, low = split_bf16(piece)
        ref[row : row + piece.shape[0], :heads] = high
        ref[row : row + piece.shape[0], heads:] = low

    keep(tails, 0, jnp.exp(end - cum) * step)
    first_mid = cum[half // 2 - 1 : half // 2, :]
    second_mid = cum[half + half // 2 - 1 : half + half // 2, :]
    middle = jnp.where(iota((tok, 1), 0) < half, first_mid, second_mid)
    keep(factors, 0, jnp.exp(cum - middle))
    keep(factors, tok, jnp.exp(middle - cum) * step)
    keep(factors, 2 * tok, jnp.exp(cum))
    keep(factors, 3 * tok, jnp.exp(second_mid - cum[:half]) * step[:half])
    keep(factors, 3 * tok + half, jnp.broadcast_to(skip_ref[...], (16, heads)))

    def columns_of(group):
        return pl.ds(pl.multiple_of(group * width, width), width)

    def build_hits(group, carry):
        hit = lax.rem(iota((2 * heads, width), 0), heads) == (
            group * per_group + iota((2 * heads, width), 1) // head_dim
        )
        hits[:, columns_of(group)] = hit.astype(F32).astype(BF16)
        return carry

    lax.fori_loop(0, GROUPS, build_hits, 0)

    def expand(rows, group):
        return jnp.dot(rows, hits[:, columns_of(group)], preferred_element_type=F32)

    ext[pad:, :inner] = x_ref[...].astype(F32)
    ext[pad:, inner:] = bc_ref[...].astype(F32)

    cache_copy.wait()
    chunk = 8
    column = iota((1, own), 1)
    target = lax.rem(column, head_dim) * heads + me * share + column // head_dim

    def pick(c, total):
        rows = jnp.concatenate([cache_all[c * chunk + i] for i in range(chunk)], axis=1)
        high, low = split_bf16(rows)
        lowest = (rows - high.astype(F32) - low.astype(F32)).astype(BF16)
        hit = iota((chunk * heads, own), 0) + c * chunk * heads == target
        hit = hit.astype(F32).astype(BF16)
        parts = jnp.dot(
            jnp.concatenate([high, low, lowest], axis=0), hit, preferred_element_type=F32
        )
        return total + (parts[:state] + parts[state : 2 * state] + parts[2 * state :])

    cache_buf[...] = lax.fori_loop(
        0, head_dim // chunk, pick, jnp.zeros((state, own), F32)
    )

    end_copy.wait()
    pair = ends[0] + ends[1]
    dsend[...] = pair
    drecv[chip] = pair

    def send_decay(d, carry):
        other, where = peer_of(d)
        remote(dsend, drecv.at[chip], d_sems, other, chip, where).start()
        return carry

    lax.fori_loop(1, chips, send_decay, 0)
    keep(tails, tok, jnp.exp(jnp.concatenate([ends[0], ends[1]], axis=0)))

    rim_copy.wait()
    rim = jnp.where(me == 0, ccache_ref[...].astype(F32), rim_recv[...].astype(F32))
    ext[pad - rim_rows : pad, :] = rim

    def conv(columns):
        total = jnp.broadcast_to(cb_ref[0:1, columns], (tok, columns.size))
        for k in range(rim_rows + 1):
            total = total + ext[pl.ds(pad - rim_rows + k, tok), columns] * cw_ref[k : k + 1, columns]
        return total * sigmoid(total)

    span = GROUPS * state
    b_all = conv(pl.ds(inner, span)).T
    for g in range(GROUPS):
        bt[g] = b_all[g * state : (g + 1) * state].astype(BF16)
    c_all = conv(pl.ds(inner + span, span)).astype(BF16)
    for g in range(GROUPS):
        cs[g] = c_all[:, g * state : (g + 1) * state]

    def p_copy(o):
        return remote(local.at[1 - core, o], pbuf.at[o], p_sems, o, o, partner)

    def a_copy(o):
        return remote(asend.at[o], abuf.at[chip], a_sems, o, chip, o * 2 + core)

    def a_wait(o):
        return remote(asend.at[o], abuf.at[o], a_sems, o, o, o * 2 + core)

    def e_copy(o):
        return remote(esend.at[o], ebuf.at[chip], e_sems, o, chip, o * 2 + core)

    def e_wait(o):
        return remote(esend.at[o], ebuf.at[o], e_sems, o, o, o * 2 + core)

    def n_copy(o):
        return remote(psend.at[o], enter.at[core, o], n_sems, o, o, partner)

    def n_wait(o):
        return remote(psend.at[o], enter.at[1 - core, o], n_sems, o, o, partner)

    def block_decay(o, of_even):
        mine = dec[core, o, 0:1, :]
        theirs = dec[core, o, 8:9, :]
        return jnp.where(even == of_even, mine, theirs)

    def block_local(o, of_even):
        return jnp.where(even == of_even, local[core, o].astype(F32), pbuf[o].astype(F32))

    def group_at(d):
        return lax.rem(home + 1 + d, GROUPS)

    def local_step(d):
        group = group_at(d)
        columns = columns_of(group)
        x = conv(columns).astype(BF16)
        xc[:, columns] = x
        tail = expand(tails[...], group)
        scaled = (x.astype(F32) * tail[:tok]).astype(BF16)
        sums = jnp.dot(bt[group], scaled, preferred_element_type=F32).astype(BF16)
        for k in range(owners):
            o = group * per_chip + k // 2
            local[k % 2, o] = sums[:, k * own : (k + 1) * own]
            dec[k % 2, o] = tail[tok:, k * own : (k + 1) * own]
        for k in range(per_chip):
            p_copy(group * per_chip + k).start()

    def pair_step(d):
        for k in range(per_chip):
            o = group_at(d) * per_chip + k
            p_copy(o).wait_recv()
            joined = block_decay(o, False) * block_local(o, True) + block_local(o, False)
            asend[o] = joined.astype(BF16)

            @pl.when(o != chip)
            def _():
                a_copy(o).start()

            @pl.when(o == chip)
            def _():
                abuf[o] = joined.astype(BF16)

    lag = 2
    for d in range(lag):
        local_step(d)

    def local_pair(d, carry):
        local_step(d)
        pair_step(d - lag)
        return carry

    lax.fori_loop(lag, GROUPS, local_pair, 0)
    for d in range(GROUPS - lag, GROUPS):
        pair_step(d)

    def diag_step(d, carry):
        group = group_at(d)
        columns = columns_of(group)
        grown = expand(factors[...], group)
        x = xc[:, columns].astype(F32)
        scaled = (x * grown[tok : 2 * tok]).astype(BF16)
        scaled_off = (x[:half] * grown[3 * tok : 3 * tok + half]).astype(BF16)
        inner_cb = jnp.dot(cs[group], bt[group], preferred_element_type=F32)
        inner_cb = jnp.where(iota((tok, tok), 0) >= iota((tok, tok), 1), inner_cb, 0.0)
        inner_cb = inner_cb.astype(BF16)
        top = jnp.dot(inner_cb[:half, :half], scaled[:half], preferred_element_type=F32)
        bottom = jnp.dot(
            inner_cb[half:],
            jnp.concatenate([scaled_off, scaled[half:]], axis=0),
            preferred_element_type=F32,
        )
        skip = grown[3 * tok + half : 3 * tok + half + 1]
        ypart[:half, columns] = top * grown[:half] + skip * x[:half]
        ypart[half:, columns] = bottom * grown[half:tok] + skip * x[half:]
        carried[:, columns] = grown[2 * tok : 3 * tok]
        z = z_ref[:, columns].astype(F32)
        zgate[:, columns] = z * sigmoid(z)
        return carry

    split = GROUPS // 2
    lax.fori_loop(0, split, diag_step, 0)

    def wait_decay(d, carry):
        other, where = peer_of(d)
        remote(dsend, drecv.at[other], d_sems, other, other, where).wait()
        return carry

    lax.fori_loop(1, chips, wait_decay, 0)
    hit = iota((heads, own), 0) == (me * share + iota((heads, own), 1) // head_dim)
    dmine[...] = jnp.dot(
        jnp.exp(drecv[:, 0, :]), hit.astype(F32), precision=HIGHEST, preferred_element_type=F32
    )

    def scan_step(s, running):
        esend[s] = running.astype(BF16)

        @pl.when(s != chip)
        def _():
            e_copy(s).start()
            a_wait(s).wait_recv()

        @pl.when(s == chip)
        def _():
            ebuf[s] = running.astype(BF16)

        return dmine[pl.ds(s, 1), :] * running + abuf[s].astype(F32)

    final = lax.fori_loop(0, chips, scan_step, cache_buf[...])
    final_ref[...] = final.T

    lax.fori_loop(split, GROUPS, diag_step, 0)

    def order(d):
        return lax.rem(home + d, GROUPS)

    def pass_step(d):
        for k in range(per_chip):
            o = order(d) * per_chip + k

            @pl.when(o != chip)
            def _():
                e_wait(o).wait_recv()

            at_even = ebuf[o]
            at_odd = block_decay(o, True) * at_even.astype(F32) + block_local(o, True)
            at_odd = at_odd.astype(BF16)
            enter[core, o] = jnp.where(even, at_even, at_odd)
            psend[o] = jnp.where(even, at_odd, at_even)
            n_copy(o).start()

    def gate_step(d):
        group = order(d)
        columns = columns_of(group)
        for k in range(per_chip):
            n_wait(group * per_chip + k).wait_recv()
        entering = jnp.concatenate(
            [enter[k % 2, group * per_chip + k // 2] for k in range(owners)], axis=1
        )
        y = ypart[:, columns] + carried[:, columns] * jnp.dot(
            cs[group], entering, preferred_element_type=F32
        )
        y = (y * live).astype(BF16).astype(F32)
        gated = y * zgate[:, columns]
        scale = lax.rsqrt(jnp.mean(gated * gated, axis=-1, keepdims=True) + 1e-05)
        out_ref[:, columns] = (gated * scale * gain_ref[0:1, columns]).astype(BF16)

    for d in range(lag):
        pass_step(d)

    def pass_gate(d, carry):
        pass_step(d)
        gate_step(d - lag)
        return carry

    lax.fori_loop(lag, GROUPS, pass_gate, 0)
    for d in range(GROUPS - lag, GROUPS):
        gate_step(d)

    def finish(o, carry):
        p_copy(o).wait_send()
        n_copy(o).wait_send()

        @pl.when(o != chip)
        def _():
            a_copy(o).wait_send()
            e_copy(o).wait_send()

        return carry

    lax.fori_loop(0, chips, finish, 0)


def body(
    devices,
    x_in,
    bc_in,
    z_in,
    dt_in,
    conv_weight,
    conv_bias,
    dt_bias,
    a_log,
    d_skip,
    norm_gain,
    conv_cache,
    cache_state,
    lengths,
):
    tok, inner = x_in.shape
    wide = inner + bc_in.shape[1]
    heads, head_dim, state = cache_state.shape
    chips = devices // 2
    share = heads // devices
    own = share * head_dim
    rim_rows = conv_cache.shape[0]
    vmem = pl.BlockSpec(memory_space=pltpu.VMEM)
    dma = pltpu.SemaphoreType.DMA
    states = pltpu.VMEM((chips, state, own), BF16)
    mixed, final = pl.pallas_call(
        functools.partial(kernel, devices),
        out_shape=(
            jax.ShapeDtypeStruct((tok, inner), BF16),
            jax.ShapeDtypeStruct((own, state), F32),
        ),
        in_specs=[pl.BlockSpec(memory_space=pltpu.SMEM)]
        + [vmem] * 11
        + [pl.BlockSpec(memory_space=pl.ANY)],
        out_specs=(vmem, vmem),
        scratch_shapes=[
            pltpu.VMEM((tok + 8, wide), F32),
            pltpu.VMEM((tok, inner), BF16),
            pltpu.VMEM((GROUPS, state, tok), BF16),
            pltpu.VMEM((GROUPS, tok, state), BF16),
            pltpu.VMEM((tok, inner), F32),
            pltpu.VMEM((tok, inner), F32),
            pltpu.VMEM((tok, inner), F32),
            pltpu.VMEM((2 * heads, inner), BF16),
            pltpu.VMEM((tok + 16, 2 * heads), BF16),
            pltpu.VMEM((3 * tok + tok // 2 + 16, 2 * heads), BF16),
            pltpu.VMEM((rim_rows, wide), BF16),
            pltpu.VMEM((rim_rows, wide), BF16),
            pltpu.VMEM((head_dim, state, heads), F32),
            pltpu.VMEM((state, own), F32),
            pltpu.VMEM((2, 8, heads), F32),
            pltpu.VMEM((8, heads), F32),
            pltpu.VMEM((chips, 8, heads), F32),
            pltpu.VMEM((2, chips, 16, own), F32),
            pltpu.VMEM((chips, own), F32),
            pltpu.VMEM((2, chips, state, own), BF16),
            states,
            states,
            states,
            states,
            states,
            states,
            pltpu.VMEM((2, chips, state, own), BF16),
            dma((2, 1)),
            dma(()),
            dma((2, 1)),
        ]
        + [dma((2, chips))] * 5,
        compiler_params=pltpu.CompilerParams(
            collective_id=0, has_side_effects=True, vmem_limit_bytes=60 * 1024 * 1024
        ),
    )(
        lengths,
        x_in,
        bc_in,
        z_in,
        dt_in,
        conv_weight,
        conv_bias[None, :],
        dt_bias[None, :],
        a_log[None, :],
        d_skip[None, :],
        norm_gain[None, :],
        conv_cache,
        jnp.transpose(cache_state, (1, 2, 0)),
    )
    return mixed, final.reshape(share, head_dim, state)


def solution(mesh):
    tokens = P(("groups", "seq"), None)
    in_specs = (
        tokens,
        tokens,
        tokens,
        tokens,
        P(),
        P(),
        P(),
        P(),
        P(),
        P(),
        P("groups", None),
        P("groups", None, None),
        P("groups"),
    )
    out_specs = (tokens, P(("groups", "seq"), None, None))
    return jax.shard_map(
        functools.partial(body, mesh.shape["seq"]),
        mesh=mesh,
        in_specs=in_specs,
        out_specs=out_specs,
        check_vma=False,
    )
```

```python
import functools

import jax
import jax.numpy as jnp
from jax import lax
from jax.experimental import pallas as pl
from jax.experimental.pallas import tpu as pltpu
from jax.sharding import PartitionSpec as P

GROUPS = 8
MESH = pl.DeviceIdType.MESH
F32 = jnp.float32
BF16 = jnp.bfloat16
HIGHEST = lax.Precision.HIGHEST


def iota(shape, dim):
    return lax.broadcasted_iota(jnp.int32, shape, dim)


def split_bf16(value):
    high = value.astype(BF16)
    return high, (value - high.astype(F32)).astype(BF16)


def sigmoid(value):
    return 0.5 * jnp.tanh(0.5 * value) + 0.5


def kernel(
    devices,
    len_ref,
    x_hbm,
    bc_hbm,
    z_hbm,
    dt_hbm,
    cw_hbm,
    cb_hbm,
    bias_hbm,
    log_hbm,
    skip_hbm,
    gain_hbm,
    ccache_hbm,
    cstate_hbm,
    out_ref,
    final_ref,
    x_ref,
    bc_ref,
    z_ref,
    dt_ref,
    cw_ref,
    cb_ref,
    bias_ref,
    log_ref,
    skip_ref,
    gain_ref,
    ccache_ref,
    ext,
    xc,
    bcv,
    bt,
    cs,
    ypart,
    zgate,
    carried,
    hits,
    tails,
    factors,
    rim_send,
    rim_recv,
    cache_all,
    cache_buf,
    ends,
    dsend,
    drecv,
    dec,
    dmine,
    local,
    pbuf,
    asend,
    abuf,
    esend,
    ebuf,
    psend,
    enter,
    rim_sem,
    in_sems,
    end_sem,
    d_sems,
    p_sems,
    a_sems,
    e_sems,
    n_sems,
):
    tok, inner = x_ref.shape
    heads = dt_ref.shape[1]
    head_dim = inner // heads
    state = bt.shape[1]
    width = inner // GROUPS
    per_group = heads // GROUPS
    chips = devices // 2
    share = heads // devices
    own = share * head_dim
    half = tok // 2
    owners = per_group // share
    per_chip = chips // GROUPS
    rim_rows = ccache_ref.shape[0]
    pad = ext.shape[0] - tok

    me = lax.axis_index("seq")
    core = lax.rem(me, 2)
    chip = me // 2
    partner = chip * 2 + 1 - core
    after = lax.rem(me + 1, devices)
    far = lax.rem(me + devices + 2 * core - 1, devices)
    even = core == 0
    home = chip // per_chip

    def remote(src, dst, sems, mine, theirs, where):
        return pltpu.make_async_remote_copy(
            src_ref=src,
            dst_ref=dst,
            send_sem=sems.at[0, mine],
            recv_sem=sems.at[1, theirs],
            device_id={"seq": where},
            device_id_type=MESH,
        )

    def peer_of(d):
        other = lax.rem(chip + d, chips)
        return other, other * 2 + core

    loads = [
        pltpu.make_async_copy(src, dst, in_sems.at[i])
        for i, (src, dst) in enumerate(
            (
                (dt_hbm, dt_ref),
                (bias_hbm, bias_ref),
                (log_hbm, log_ref),
                (x_hbm, x_ref),
                (bc_hbm, bc_ref),
                (cw_hbm, cw_ref),
                (cb_hbm, cb_ref),
                (ccache_hbm, ccache_ref),
                (skip_hbm, skip_ref),
                (cstate_hbm, cache_all),
                (z_hbm, z_ref),
                (gain_hbm, gain_ref),
            )
        )
    ]
    for load in loads:
        load.start()

    barrier = pltpu.get_barrier_semaphore()
    for other in (partner, far):
        pl.semaphore_signal(barrier, inc=1, device_id={"seq": other}, device_id_type=MESH)

    def greet(d, carry):
        pl.semaphore_signal(
            barrier, inc=1, device_id={"seq": peer_of(d)[1]}, device_id_type=MESH
        )
        return carry

    lax.fori_loop(1, chips, greet, 0)
    for load in loads[:3]:
        load.wait()

    live = (iota((tok, 1), 0) + me * tok < len_ref[0]).astype(F32)
    raw = dt_ref[...].astype(F32) + bias_ref[...]
    step = (jnp.maximum(raw, 0.0) + jnp.log1p(jnp.exp(-jnp.abs(raw)))) * live
    rate = -jnp.exp(log_ref[...]) * step
    lower = (iota((tok, tok), 0) >= iota((tok, tok), 1)).astype(F32)
    cum = jnp.dot(lower, rate, precision=HIGHEST, preferred_element_type=F32)
    end = cum[tok - 1 : tok, :]
    ends[0] = jnp.broadcast_to(end, ends.shape[1:])
    for load in loads[3:5]:
        load.wait()
    rim_send[:, :inner] = x_ref[tok - rim_rows :, :]
    rim_send[:, inner:] = bc_ref[tok - rim_rows :, :]

    pl.semaphore_wait(barrier, chips + 1)
    rim_copy = remote(rim_send, rim_recv, rim_sem, 0, 0, after)
    rim_copy.start()
    end_copy = remote(ends.at[0], ends.at[1], end_sem, 0, 0, partner)
    end_copy.start()

    def keep(ref, row, piece):
        high, low = split_bf16(piece)
        ref[row : row + piece.shape[0], :heads] = high
        ref[row : row + piece.shape[0], heads:] = low

    keep(tails, 0, jnp.exp(end - cum) * step)
    def columns_of(group):
        return pl.ds(pl.multiple_of(group * width, width), width)

    def expand(rows, group):
        return jnp.dot(rows, hits[:, columns_of(group)], preferred_element_type=F32)

    ext[pad:, :inner] = x_ref[...].astype(F32)
    ext[pad:, inner:] = bc_ref[...].astype(F32)

    for load in loads[5:8]:
        load.wait()

    def conv(columns, row, rows):
        total = jnp.broadcast_to(cb_ref[0:1, columns], (rows, columns.size))
        for k in range(rim_rows + 1):
            seen = ext[pl.ds(pad - rim_rows + k + row, rows), columns]
            total = total + seen * cw_ref[k : k + 1, columns]
        return total * sigmoid(total)

    first = 16
    chunks = [(first, 16)] + [(row, 32) for row in range(2 * first, tok, 32)]

    def conv_step(group, carry):
        columns = columns_of(group)
        hit = lax.rem(iota((2 * heads, width), 0), heads) == (
            group * per_group + iota((2 * heads, width), 1) // head_dim
        )
        hits[:, columns] = hit.astype(F32).astype(BF16)
        for row, rows in chunks:
            xc[row : row + rows, columns] = conv(columns, row, rows).astype(BF16)
        return carry

    lax.fori_loop(0, GROUPS, conv_step, 0)
    span = GROUPS * state
    sides = (pl.ds(inner, span), pl.ds(inner + span, span))
    for side, columns in enumerate(sides):
        for row, rows in chunks:
            bcv[side, row : row + rows] = conv(columns, row, rows)

    end_copy.wait()
    pair = ends[0] + ends[1]
    dsend[...] = pair
    drecv[chip] = pair

    def send_decay(d, carry):
        other, where = peer_of(d)
        remote(dsend, drecv.at[chip], d_sems, other, chip, where).start()
        return carry

    lax.fori_loop(1, chips, send_decay, 0)
    keep(tails, tok, jnp.exp(jnp.concatenate([ends[0], ends[1]], axis=0)))

    rim_copy.wait()
    rim = jnp.where(me == 0, ccache_ref[...].astype(F32), rim_recv[...].astype(F32))
    ext[pad - rim_rows : pad, :] = rim

    for side, columns in enumerate(sides):
        bcv[side, :first] = conv(columns, 0, first)
    b_all = bcv[0].T
    for g in range(GROUPS):
        bt[g] = b_all[g * state : (g + 1) * state].astype(BF16)
    c_all = bcv[1].astype(BF16)
    for g in range(GROUPS):
        cs[g] = c_all[:, g * state : (g + 1) * state]

    def p_copy(o):
        return remote(local.at[1 - core, o], pbuf.at[o], p_sems, o, o, partner)

    def a_copy(o):
        return remote(asend.at[o], abuf.at[chip], a_sems, o, chip, o * 2 + core)

    def a_wait(o):
        return remote(asend.at[o], abuf.at[o], a_sems, o, o, o * 2 + core)

    def e_copy(o):
        return remote(esend.at[o], ebuf.at[chip], e_sems, o, chip, o * 2 + core)

    def e_wait(o):
        return remote(esend.at[o], ebuf.at[o], e_sems, o, o, o * 2 + core)

    def n_copy(o):
        return remote(psend.at[o], enter.at[core, o], n_sems, o, o, partner)

    def n_wait(o):
        return remote(psend.at[o], enter.at[1 - core, o], n_sems, o, o, partner)

    def block_decay(o, of_even):
        mine = dec[core, o, 0:1, :]
        theirs = dec[core, o, 8:9, :]
        return jnp.where(even == of_even, mine, theirs)

    def block_local(o, of_even):
        return jnp.where(even == of_even, local[core, o].astype(F32), pbuf[o].astype(F32))

    def group_at(d):
        return lax.rem(home + 1 + d, GROUPS)

    def local_step(d):
        group = group_at(d)
        columns = columns_of(group)
        xc[:first, columns] = conv(columns, 0, first).astype(BF16)
        x = xc[:, columns]
        tail = expand(tails[...], group)
        scaled = (x.astype(F32) * tail[:tok]).astype(BF16)
        sums = jnp.dot(bt[group], scaled, preferred_element_type=F32).astype(BF16)
        for k in range(owners):
            o = group * per_chip + k // 2
            local[k % 2, o] = sums[:, k * own : (k + 1) * own]
            dec[k % 2, o] = tail[tok:, k * own : (k + 1) * own]
        for k in range(per_chip):
            p_copy(group * per_chip + k).start()

    def pair_step(d):
        for k in range(per_chip):
            o = group_at(d) * per_chip + k
            p_copy(o).wait_recv()
            joined = block_decay(o, False) * block_local(o, True) + block_local(o, False)
            asend[o] = joined.astype(BF16)

            @pl.when(o != chip)
            def _():
                a_copy(o).start()

            @pl.when(o == chip)
            def _():
                abuf[o] = joined.astype(BF16)

    lag = 2
    for d in range(lag):
        local_step(d)

    def local_pair(d, carry):
        local_step(d)
        pair_step(d - lag)
        return carry

    lax.fori_loop(lag, GROUPS, local_pair, 0)
    for d in range(GROUPS - lag, GROUPS):
        pair_step(d)

    for load in loads[8:]:
        load.wait()

    first_mid = cum[half // 2 - 1 : half // 2, :]
    second_mid = cum[half + half // 2 - 1 : half + half // 2, :]
    middle = jnp.where(iota((tok, 1), 0) < half, first_mid, second_mid)
    keep(factors, 0, jnp.exp(cum - middle))
    keep(factors, tok, jnp.exp(middle - cum) * step)
    keep(factors, 2 * tok, jnp.exp(cum))
    keep(factors, 3 * tok, jnp.exp(second_mid - cum[:half]) * step[:half])
    keep(factors, 3 * tok + half, jnp.broadcast_to(skip_ref[...], (16, heads)))

    def diag_step(d, carry):
        group = group_at(d)
        columns = columns_of(group)
        grown = expand(factors[...], group)
        x = xc[:, columns].astype(F32)
        scaled = (x * grown[tok : 2 * tok]).astype(BF16)
        scaled_off = (x[:half] * grown[3 * tok : 3 * tok + half]).astype(BF16)
        inner_cb = jnp.dot(cs[group], bt[group], preferred_element_type=F32)
        inner_cb = jnp.where(iota((tok, tok), 0) >= iota((tok, tok), 1), inner_cb, 0.0)
        inner_cb = inner_cb.astype(BF16)
        top = jnp.dot(inner_cb[:half, :half], scaled[:half], preferred_element_type=F32)
        bottom = jnp.dot(
            inner_cb[half:],
            jnp.concatenate([scaled_off, scaled[half:]], axis=0),
            preferred_element_type=F32,
        )
        skip = grown[3 * tok + half : 3 * tok + half + 1]
        ypart[:half, columns] = top * grown[:half] + skip * x[:half]
        ypart[half:, columns] = bottom * grown[half:tok] + skip * x[half:]
        carried[:, columns] = grown[2 * tok : 3 * tok]
        z = z_ref[:, columns].astype(F32)
        zgate[:, columns] = z * sigmoid(z)
        return carry

    split = GROUPS // 2
    lax.fori_loop(0, split, diag_step, 0)

    chunk = 8
    column = iota((1, own), 1)
    target = lax.rem(column, head_dim) * heads + me * share + column // head_dim

    def pick(c, total):
        rows = jnp.concatenate([cache_all[c * chunk + i] for i in range(chunk)], axis=1)
        high, low = split_bf16(rows)
        lowest = (rows - high.astype(F32) - low.astype(F32)).astype(BF16)
        hit = iota((chunk * heads, own), 0) + c * chunk * heads == target
        hit = hit.astype(F32).astype(BF16)
        parts = jnp.dot(
            jnp.concatenate([high, low, lowest], axis=0), hit, preferred_element_type=F32
        )
        return total + (parts[:state] + parts[state : 2 * state] + parts[2 * state :])

    cache_buf[...] = lax.fori_loop(
        0, head_dim // chunk, pick, jnp.zeros((state, own), F32)
    )

    def wait_decay(d, carry):
        other, where = peer_of(d)
        remote(dsend, drecv.at[other], d_sems, other, other, where).wait()
        return carry

    lax.fori_loop(1, chips, wait_decay, 0)
    hit = iota((heads, own), 0) == (me * share + iota((heads, own), 1) // head_dim)
    dmine[...] = jnp.dot(
        jnp.exp(drecv[:, 0, :]), hit.astype(F32), precision=HIGHEST, preferred_element_type=F32
    )

    def scan_step(s, running):
        esend[s] = running.astype(BF16)

        @pl.when(s != chip)
        def _():
            e_copy(s).start()
            a_wait(s).wait_recv()

        @pl.when(s == chip)
        def _():
            ebuf[s] = running.astype(BF16)

        return dmine[pl.ds(s, 1), :] * running + abuf[s].astype(F32)

    final = lax.fori_loop(0, chips, scan_step, cache_buf[...])
    final_ref[...] = final.T

    lax.fori_loop(split, GROUPS, diag_step, 0)

    def order(d):
        return lax.rem(home + d, GROUPS)

    def pass_step(d):
        for k in range(per_chip):
            o = order(d) * per_chip + k

            @pl.when(o != chip)
            def _():
                e_wait(o).wait_recv()

            at_even = ebuf[o]
            at_odd = block_decay(o, True) * at_even.astype(F32) + block_local(o, True)
            at_odd = at_odd.astype(BF16)
            enter[core, o] = jnp.where(even, at_even, at_odd)
            psend[o] = jnp.where(even, at_odd, at_even)
            n_copy(o).start()

    def gate_step(d):
        group = order(d)
        columns = columns_of(group)
        for k in range(per_chip):
            n_wait(group * per_chip + k).wait_recv()
        entering = jnp.concatenate(
            [enter[k % 2, group * per_chip + k // 2] for k in range(owners)], axis=1
        )
        y = ypart[:, columns] + carried[:, columns] * jnp.dot(
            cs[group], entering, preferred_element_type=F32
        )
        y = (y * live).astype(BF16).astype(F32)
        gated = y * zgate[:, columns]
        scale = lax.rsqrt(jnp.mean(gated * gated, axis=-1, keepdims=True) + 1e-05)
        out_ref[:, columns] = (gated * scale * gain_ref[0:1, columns]).astype(BF16)

    for d in range(lag):
        pass_step(d)

    def pass_gate(d, carry):
        pass_step(d)
        gate_step(d - lag)
        return carry

    lax.fori_loop(lag, GROUPS, pass_gate, 0)
    for d in range(GROUPS - lag, GROUPS):
        gate_step(d)

    def finish(o, carry):
        p_copy(o).wait_send()
        n_copy(o).wait_send()

        @pl.when(o != chip)
        def _():
            a_copy(o).wait_send()
            e_copy(o).wait_send()

        return carry

    lax.fori_loop(0, chips, finish, 0)


def body(
    devices,
    x_in,
    bc_in,
    z_in,
    dt_in,
    conv_weight,
    conv_bias,
    dt_bias,
    a_log,
    d_skip,
    norm_gain,
    conv_cache,
    cache_state,
    lengths,
):
    tok, inner = x_in.shape
    wide = inner + bc_in.shape[1]
    heads, head_dim, state = cache_state.shape
    chips = devices // 2
    share = heads // devices
    own = share * head_dim
    rim_rows = conv_cache.shape[0]
    vmem = pl.BlockSpec(memory_space=pltpu.VMEM)
    dma = pltpu.SemaphoreType.DMA
    states = pltpu.VMEM((chips, state, own), BF16)
    arrays = (
        x_in,
        bc_in,
        z_in,
        dt_in,
        conv_weight,
        conv_bias[None, :],
        dt_bias[None, :],
        a_log[None, :],
        d_skip[None, :],
        norm_gain[None, :],
        conv_cache,
        jnp.transpose(cache_state, (1, 2, 0)),
    )
    mixed, final = pl.pallas_call(
        functools.partial(kernel, devices),
        out_shape=(
            jax.ShapeDtypeStruct((tok, inner), BF16),
            jax.ShapeDtypeStruct((own, state), F32),
        ),
        in_specs=[pl.BlockSpec(memory_space=pltpu.SMEM)]
        + [pl.BlockSpec(memory_space=pltpu.HBM)] * len(arrays),
        out_specs=(vmem, vmem),
        scratch_shapes=[pltpu.VMEM(a.shape, a.dtype) for a in arrays[:-1]]
        + [
            pltpu.VMEM((tok + 8, wide), F32),
            pltpu.VMEM((tok, inner), BF16),
            pltpu.VMEM((2, tok, GROUPS * state), F32),
            pltpu.VMEM((GROUPS, state, tok), BF16),
            pltpu.VMEM((GROUPS, tok, state), BF16),
            pltpu.VMEM((tok, inner), F32),
            pltpu.VMEM((tok, inner), F32),
            pltpu.VMEM((tok, inner), F32),
            pltpu.VMEM((2 * heads, inner), BF16),
            pltpu.VMEM((tok + 16, 2 * heads), BF16),
            pltpu.VMEM((3 * tok + tok // 2 + 16, 2 * heads), BF16),
            pltpu.VMEM((rim_rows, wide), BF16),
            pltpu.VMEM((rim_rows, wide), BF16),
            pltpu.VMEM((head_dim, state, heads), F32),
            pltpu.VMEM((state, own), F32),
            pltpu.VMEM((2, 8, heads), F32),
            pltpu.VMEM((8, heads), F32),
            pltpu.VMEM((chips, 8, heads), F32),
            pltpu.VMEM((2, chips, 16, own), F32),
            pltpu.VMEM((chips, own), F32),
            pltpu.VMEM((2, chips, state, own), BF16),
            states,
            states,
            states,
            states,
            states,
            states,
            pltpu.VMEM((2, chips, state, own), BF16),
            dma((2, 1)),
            dma((len(arrays),)),
            dma((2, 1)),
        ]
        + [dma((2, chips))] * 5,
        compiler_params=pltpu.CompilerParams(
            collective_id=0, has_side_effects=True, vmem_limit_bytes=60 * 1024 * 1024
        ),
    )(lengths, *arrays)
    return mixed, final.reshape(share, head_dim, state)


def solution(mesh):
    tokens = P(("groups", "seq"), None)
    in_specs = (
        tokens,
        tokens,
        tokens,
        tokens,
        P(),
        P(),
        P(),
        P(),
        P(),
        P(),
        P("groups", None),
        P("groups", None, None),
        P("groups"),
    )
    out_specs = (tokens, P(("groups", "seq"), None, None))
    return jax.shard_map(
        functools.partial(body, mesh.shape["seq"]),
        mesh=mesh,
        in_specs=in_specs,
        out_specs=out_specs,
        check_vma=False,
    )
```

```python
import functools

import jax
import jax.numpy as jnp
from jax import lax
from jax.experimental import pallas as pl
from jax.experimental.pallas import tpu as pltpu
from jax.sharding import PartitionSpec as P

GROUPS = 8
MESH = pl.DeviceIdType.MESH
F32 = jnp.float32
BF16 = jnp.bfloat16
HIGHEST = lax.Precision.HIGHEST


def iota(shape, dim):
    return lax.broadcasted_iota(jnp.int32, shape, dim)


def split_bf16(value):
    high = value.astype(BF16)
    return high, (value - high.astype(F32)).astype(BF16)


def sigmoid(value):
    return 0.5 * jnp.tanh(0.5 * value) + 0.5


def kernel(
    devices,
    len_ref,
    x_hbm,
    bc_hbm,
    z_hbm,
    dt_hbm,
    cw_hbm,
    cb_hbm,
    bias_hbm,
    log_hbm,
    skip_hbm,
    gain_hbm,
    ccache_hbm,
    cstate_hbm,
    out_ref,
    final_ref,
    x_ref,
    bc_ref,
    z_ref,
    dt_ref,
    cw_ref,
    cb_ref,
    bias_ref,
    log_ref,
    skip_ref,
    gain_ref,
    ccache_ref,
    ext,
    xc,
    bcv,
    bt,
    cs,
    ypart,
    zgate,
    carried,
    hits,
    tails,
    factors,
    rim_send,
    rim_recv,
    cache_all,
    cache_buf,
    ends,
    dsend,
    drecv,
    dec,
    dmine,
    local,
    pbuf,
    asend,
    abuf,
    esend,
    ebuf,
    psend,
    enter,
    rim_sem,
    in_sems,
    end_sem,
    d_sems,
    p_sems,
    a_sems,
    e_sems,
    n_sems,
):
    tok, inner = x_ref.shape
    heads = dt_ref.shape[1]
    head_dim = inner // heads
    state = bt.shape[1]
    width = inner // GROUPS
    per_group = heads // GROUPS
    chips = devices // 2
    share = heads // devices
    own = share * head_dim
    half = tok // 2
    owners = per_group // share
    per_chip = chips // GROUPS
    rim_rows = ccache_ref.shape[0]
    pad = ext.shape[0] - tok

    me = lax.axis_index("seq")
    core = lax.rem(me, 2)
    chip = me // 2
    partner = chip * 2 + 1 - core
    after = lax.rem(me + 1, devices)
    far = lax.rem(me + devices + 2 * core - 1, devices)
    even = core == 0
    home = chip // per_chip

    def remote(src, dst, sems, mine, theirs, where):
        return pltpu.make_async_remote_copy(
            src_ref=src,
            dst_ref=dst,
            send_sem=sems.at[0, mine],
            recv_sem=sems.at[1, theirs],
            device_id={"seq": where},
            device_id_type=MESH,
        )

    def peer_of(d):
        other = lax.rem(chip + d, chips)
        return other, other * 2 + core

    loads = [
        pltpu.make_async_copy(src, dst, in_sems.at[i])
        for i, (src, dst) in enumerate(
            (
                (dt_hbm, dt_ref),
                (bias_hbm, bias_ref),
                (log_hbm, log_ref),
                (x_hbm, x_ref),
                (bc_hbm, bc_ref),
                (cw_hbm, cw_ref),
                (cb_hbm, cb_ref),
                (ccache_hbm, ccache_ref),
                (skip_hbm, skip_ref),
                (cstate_hbm, cache_all),
                (z_hbm, z_ref),
                (gain_hbm, gain_ref),
            )
        )
    ]
    for load in loads:
        load.start()

    barrier = pltpu.get_barrier_semaphore()
    for other in (partner, far):
        pl.semaphore_signal(barrier, inc=1, device_id={"seq": other}, device_id_type=MESH)

    def greet(d, carry):
        pl.semaphore_signal(
            barrier, inc=1, device_id={"seq": peer_of(d)[1]}, device_id_type=MESH
        )
        return carry

    lax.fori_loop(1, chips, greet, 0)
    for load in loads[:3]:
        load.wait()

    live = (iota((tok, 1), 0) + me * tok < len_ref[0]).astype(F32)
    raw = dt_ref[...].astype(F32) + bias_ref[...]
    step = (jnp.maximum(raw, 0.0) + jnp.log1p(jnp.exp(-jnp.abs(raw)))) * live
    rate = -jnp.exp(log_ref[...]) * step
    lower = (iota((tok, tok), 0) >= iota((tok, tok), 1)).astype(F32)
    cum = jnp.dot(lower, rate, precision=HIGHEST, preferred_element_type=F32)
    end = cum[tok - 1 : tok, :]
    ends[0] = jnp.broadcast_to(end, ends.shape[1:])
    for load in loads[3:5]:
        load.wait()
    rim_send[:, :inner] = x_ref[tok - rim_rows :, :]
    rim_send[:, inner:] = bc_ref[tok - rim_rows :, :]

    pl.semaphore_wait(barrier, chips + 1)
    rim_copy = remote(rim_send, rim_recv, rim_sem, 0, 0, after)
    rim_copy.start()
    end_copy = remote(ends.at[0], ends.at[1], end_sem, 0, 0, partner)
    end_copy.start()

    def keep(ref, row, piece):
        high, low = split_bf16(piece)
        ref[row : row + piece.shape[0], :heads] = high
        ref[row : row + piece.shape[0], heads:] = low

    keep(tails, 0, jnp.exp(end - cum) * step)
    def columns_of(group):
        return pl.ds(pl.multiple_of(group * width, width), width)

    def expand(rows, group):
        return jnp.dot(rows, hits[:, columns_of(group)], preferred_element_type=F32)

    ext[pad:, :inner] = x_ref[...].astype(F32)
    ext[pad:, inner:] = bc_ref[...].astype(F32)

    for load in loads[5:8]:
        load.wait()

    def conv(columns, row, rows):
        total = jnp.broadcast_to(cb_ref[0:1, columns], (rows, columns.size))
        for k in range(rim_rows + 1):
            seen = ext[pl.ds(pad - rim_rows + k + row, rows), columns]
            total = total + seen * cw_ref[k : k + 1, columns]
        return total * sigmoid(total)

    first = 16
    chunks = [(first, 16)] + [(row, 32) for row in range(2 * first, tok, 32)]

    def conv_step(group, carry):
        columns = columns_of(group)
        hit = lax.rem(iota((2 * heads, width), 0), heads) == (
            group * per_group + iota((2 * heads, width), 1) // head_dim
        )
        hits[:, columns] = hit.astype(F32).astype(BF16)
        for row, rows in chunks:
            xc[row : row + rows, columns] = conv(columns, row, rows).astype(BF16)
        return carry

    lax.fori_loop(0, GROUPS, conv_step, 0)
    span = GROUPS * state
    sides = (pl.ds(inner, span), pl.ds(inner + span, span))
    for side, columns in enumerate(sides):
        for row, rows in chunks:
            bcv[side, row : row + rows] = conv(columns, row, rows)

    end_copy.wait()
    pair = ends[0] + ends[1]
    dsend[...] = pair
    drecv[chip] = pair

    def send_decay(d, carry):
        other, where = peer_of(d)
        remote(dsend, drecv.at[chip], d_sems, other, chip, where).start()
        return carry

    lax.fori_loop(1, chips, send_decay, 0)
    keep(tails, tok, jnp.exp(jnp.concatenate([ends[0], ends[1]], axis=0)))

    rim_copy.wait()
    rim = jnp.where(me == 0, ccache_ref[...].astype(F32), rim_recv[...].astype(F32))
    ext[pad - rim_rows : pad, :] = rim

    for side, columns in enumerate(sides):
        bcv[side, :first] = conv(columns, 0, first)
    b_all = bcv[0].T
    for g in range(GROUPS):
        bt[g] = b_all[g * state : (g + 1) * state].astype(BF16)
    c_all = bcv[1].astype(BF16)
    for g in range(GROUPS):
        cs[g] = c_all[:, g * state : (g + 1) * state]

    def p_copy(o):
        return remote(local.at[1 - core, o], pbuf.at[o], p_sems, o, o, partner)

    def a_copy(o):
        return remote(asend.at[o], abuf.at[chip], a_sems, o, chip, o * 2 + core)

    def a_wait(o):
        return remote(asend.at[o], abuf.at[o], a_sems, o, o, o * 2 + core)

    def e_copy(o):
        return remote(esend.at[o], ebuf.at[chip], e_sems, o, chip, o * 2 + core)

    def e_wait(o):
        return remote(esend.at[o], ebuf.at[o], e_sems, o, o, o * 2 + core)

    def n_copy(o):
        return remote(psend.at[o], enter.at[core, o], n_sems, o, o, partner)

    def n_wait(o):
        return remote(psend.at[o], enter.at[1 - core, o], n_sems, o, o, partner)

    def block_decay(o, of_even):
        mine = dec[core, o, 0:1, :]
        theirs = dec[core, o, 8:9, :]
        return jnp.where(even == of_even, mine, theirs)

    def block_local(o, of_even):
        return jnp.where(even == of_even, local[core, o].astype(F32), pbuf[o].astype(F32))

    def group_at(d):
        return lax.rem(home + 1 + d, GROUPS)

    def local_step(d):
        group = group_at(d)
        columns = columns_of(group)
        xc[:first, columns] = conv(columns, 0, first).astype(BF16)
        x = xc[:, columns]
        tail = expand(tails[...], group)
        scaled = (x.astype(F32) * tail[:tok]).astype(BF16)
        sums = jnp.dot(bt[group], scaled, preferred_element_type=F32).astype(BF16)
        for k in range(owners):
            o = group * per_chip + k // 2
            local[k % 2, o] = sums[:, k * own : (k + 1) * own]
            dec[k % 2, o] = tail[tok:, k * own : (k + 1) * own]
        for k in range(per_chip):
            p_copy(group * per_chip + k).start()

    def pair_step(d):
        for k in range(per_chip):
            o = group_at(d) * per_chip + k
            p_copy(o).wait_recv()
            joined = block_decay(o, False) * block_local(o, True) + block_local(o, False)
            asend[o] = joined.astype(BF16)

            @pl.when(o != chip)
            def _():
                a_copy(o).start()

            @pl.when(o == chip)
            def _():
                abuf[o] = joined.astype(BF16)

    lag = 2
    for d in range(lag):
        local_step(d)

    def local_pair(d, carry):
        local_step(d)
        pair_step(d - lag)
        return carry

    lax.fori_loop(lag, GROUPS, local_pair, 0)
    for d in range(GROUPS - lag, GROUPS):
        pair_step(d)

    for load in loads[8:]:
        load.wait()

    first_mid = cum[half // 2 - 1 : half // 2, :]
    second_mid = cum[half + half // 2 - 1 : half + half // 2, :]
    middle = jnp.where(iota((tok, 1), 0) < half, first_mid, second_mid)
    keep(factors, 0, jnp.exp(cum - middle))
    keep(factors, tok, jnp.exp(middle - cum) * step)
    keep(factors, 2 * tok, jnp.exp(cum))
    keep(factors, 3 * tok, jnp.exp(second_mid - cum[:half]) * step[:half])
    keep(factors, 3 * tok + half, jnp.broadcast_to(skip_ref[...], (16, heads)))

    def diag_step(d, carry):
        group = group_at(d)
        columns = columns_of(group)
        grown = expand(factors[...], group)
        x = xc[:, columns].astype(F32)
        scaled = (x * grown[tok : 2 * tok]).astype(BF16)
        scaled_off = (x[:half] * grown[3 * tok : 3 * tok + half]).astype(BF16)
        inner_cb = jnp.dot(cs[group], bt[group], preferred_element_type=F32)
        inner_cb = jnp.where(iota((tok, tok), 0) >= iota((tok, tok), 1), inner_cb, 0.0)
        inner_cb = inner_cb.astype(BF16)
        top = jnp.dot(inner_cb[:half, :half], scaled[:half], preferred_element_type=F32)
        bottom = jnp.dot(
            inner_cb[half:],
            jnp.concatenate([scaled_off, scaled[half:]], axis=0),
            preferred_element_type=F32,
        )
        skip = grown[3 * tok + half : 3 * tok + half + 1]
        ypart[:half, columns] = top * grown[:half] + skip * x[:half]
        ypart[half:, columns] = bottom * grown[half:tok] + skip * x[half:]
        carried[:, columns] = grown[2 * tok : 3 * tok]
        z = z_ref[:, columns].astype(F32)
        zgate[:, columns] = z * sigmoid(z)
        return carry

    split = GROUPS // 2
    lax.fori_loop(0, split, diag_step, 0)

    chunk = 8
    column = iota((1, own), 1)
    target = lax.rem(column, head_dim) * heads + me * share + column // head_dim

    def pick(c, total):
        rows = jnp.concatenate([cache_all[c * chunk + i] for i in range(chunk)], axis=1)
        high, low = split_bf16(rows)
        lowest = (rows - high.astype(F32) - low.astype(F32)).astype(BF16)
        hit = iota((chunk * heads, own), 0) + c * chunk * heads == target
        hit = hit.astype(F32).astype(BF16)
        parts = jnp.dot(
            jnp.concatenate([high, low, lowest], axis=0), hit, preferred_element_type=F32
        )
        return total + (parts[:state] + parts[state : 2 * state] + parts[2 * state :])

    cache_buf[...] = lax.fori_loop(
        0, head_dim // chunk, pick, jnp.zeros((state, own), F32)
    )

    def wait_decay(d, carry):
        other, where = peer_of(d)
        remote(dsend, drecv.at[other], d_sems, other, other, where).wait()
        return carry

    lax.fori_loop(1, chips, wait_decay, 0)
    hit = iota((heads, own), 0) == (me * share + iota((heads, own), 1) // head_dim)
    dmine[...] = jnp.dot(
        jnp.exp(drecv[:, 0, :]), hit.astype(F32), precision=HIGHEST, preferred_element_type=F32
    )

    def scan_step(s, running):
        esend[s] = running.astype(BF16)

        @pl.when(s != chip)
        def _():
            e_copy(s).start()
            a_wait(s).wait_recv()

        @pl.when(s == chip)
        def _():
            ebuf[s] = running.astype(BF16)

        return dmine[pl.ds(s, 1), :] * running + abuf[s].astype(F32)

    final = lax.fori_loop(0, chips, scan_step, cache_buf[...])
    final_ref[...] = final.T

    lax.fori_loop(split, GROUPS, diag_step, 0)

    def order(d):
        return lax.rem(home + d, GROUPS)

    def pass_step(d):
        for k in range(per_chip):
            o = order(d) * per_chip + k

            @pl.when(o != chip)
            def _():
                e_wait(o).wait_recv()

            at_even = ebuf[o]
            at_odd = block_decay(o, True) * at_even.astype(F32) + block_local(o, True)
            at_odd = at_odd.astype(BF16)
            enter[core, o] = jnp.where(even, at_even, at_odd)
            psend[o] = jnp.where(even, at_odd, at_even)
            n_copy(o).start()

    def gate_step(d):
        group = order(d)
        columns = columns_of(group)
        for k in range(per_chip):
            n_wait(group * per_chip + k).wait_recv()
        entering = jnp.concatenate(
            [enter[k % 2, group * per_chip + k // 2] for k in range(owners)], axis=1
        )
        y = ypart[:, columns] + carried[:, columns] * jnp.dot(
            cs[group], entering, preferred_element_type=F32
        )
        y = (y * live).astype(BF16).astype(F32)
        gated = y * zgate[:, columns]
        scale = lax.rsqrt(jnp.mean(gated * gated, axis=-1, keepdims=True) + 1e-05)
        out_ref[:, columns] = (gated * scale * gain_ref[0:1, columns]).astype(BF16)

    for d in range(lag):
        pass_step(d)

    def pass_gate(d, carry):
        pass_step(d)
        gate_step(d - lag)
        return carry

    lax.fori_loop(lag, GROUPS, pass_gate, 0)
    for d in range(GROUPS - lag, GROUPS):
        gate_step(d)

    def finish(o, carry):
        p_copy(o).wait_send()
        n_copy(o).wait_send()

        @pl.when(o != chip)
        def _():
            a_copy(o).wait_send()
            e_copy(o).wait_send()

        return carry

    lax.fori_loop(0, chips, finish, 0)


def body(
    devices,
    x_in,
    bc_in,
    z_in,
    dt_in,
    conv_weight,
    conv_bias,
    dt_bias,
    a_log,
    d_skip,
    norm_gain,
    conv_cache,
    cache_state,
    lengths,
):
    tok, inner = x_in.shape
    wide = inner + bc_in.shape[1]
    heads, head_dim, state = cache_state.shape
    chips = devices // 2
    share = heads // devices
    own = share * head_dim
    rim_rows = conv_cache.shape[0]
    vmem = pl.BlockSpec(memory_space=pltpu.VMEM)
    dma = pltpu.SemaphoreType.DMA
    states = pltpu.VMEM((chips, state, own), BF16)
    arrays = (
        x_in,
        bc_in,
        z_in,
        dt_in,
        conv_weight,
        conv_bias[None, :],
        dt_bias[None, :],
        a_log[None, :],
        d_skip[None, :],
        norm_gain[None, :],
        conv_cache,
        jnp.transpose(cache_state, (1, 2, 0)),
    )
    arrays = tuple(pltpu.with_memory_space_constraint(a, pltpu.HBM) for a in arrays)
    mixed, final = pl.pallas_call(
        functools.partial(kernel, devices),
        out_shape=(
            jax.ShapeDtypeStruct((tok, inner), BF16),
            jax.ShapeDtypeStruct((own, state), F32),
        ),
        in_specs=[pl.BlockSpec(memory_space=pltpu.SMEM)]
        + [pl.BlockSpec(memory_space=pltpu.HBM)] * len(arrays),
        out_specs=(vmem, vmem),
        scratch_shapes=[pltpu.VMEM(a.shape, a.dtype) for a in arrays[:-1]]
        + [
            pltpu.VMEM((tok + 8, wide), F32),
            pltpu.VMEM((tok, inner), BF16),
            pltpu.VMEM((2, tok, GROUPS * state), F32),
            pltpu.VMEM((GROUPS, state, tok), BF16),
            pltpu.VMEM((GROUPS, tok, state), BF16),
            pltpu.VMEM((tok, inner), F32),
            pltpu.VMEM((tok, inner), F32),
            pltpu.VMEM((tok, inner), F32),
            pltpu.VMEM((2 * heads, inner), BF16),
            pltpu.VMEM((tok + 16, 2 * heads), BF16),
            pltpu.VMEM((3 * tok + tok // 2 + 16, 2 * heads), BF16),
            pltpu.VMEM((rim_rows, wide), BF16),
            pltpu.VMEM((rim_rows, wide), BF16),
            pltpu.VMEM((head_dim, state, heads), F32),
            pltpu.VMEM((state, own), F32),
            pltpu.VMEM((2, 8, heads), F32),
            pltpu.VMEM((8, heads), F32),
            pltpu.VMEM((chips, 8, heads), F32),
            pltpu.VMEM((2, chips, 16, own), F32),
            pltpu.VMEM((chips, own), F32),
            pltpu.VMEM((2, chips, state, own), BF16),
            states,
            states,
            states,
            states,
            states,
            states,
            pltpu.VMEM((2, chips, state, own), BF16),
            dma((2, 1)),
            dma((len(arrays),)),
            dma((2, 1)),
        ]
        + [dma((2, chips))] * 5,
        compiler_params=pltpu.CompilerParams(
            collective_id=0, has_side_effects=True, vmem_limit_bytes=44 * 1024 * 1024
        ),
    )(lengths, *arrays)
    return mixed, final.reshape(share, head_dim, state)


def solution(mesh):
    tokens = P(("groups", "seq"), None)
    in_specs = (
        tokens,
        tokens,
        tokens,
        tokens,
        P(),
        P(),
        P(),
        P(),
        P(),
        P(),
        P("groups", None),
        P("groups", None, None),
        P("groups"),
    )
    out_specs = (tokens, P(("groups", "seq"), None, None))
    return jax.shard_map(
        functools.partial(body, mesh.shape["seq"]),
        mesh=mesh,
        in_specs=in_specs,
        out_specs=out_specs,
        check_vma=False,
    )
```
